512 devices in a mesh: seq: 64 (over y, x, core), head: 8 (over z).
Axes of the slice: x: 4, y: 8, z: 8, core: 2. Of those that a mesh axis runs over, the one named last changes fastest.
Arguments:
- queries: bfloat16 [8192, 6144], P('seq', 'head'), may hold values from -6 to 6
- key_vectors: bfloat16 [8192, 6144], P('seq', 'head'), may hold values from -6 to 6
- value_vectors: bfloat16 [8192, 6144], P('seq', 'head'), may hold values from -6 to 6
- norm_gain: float32 [6144], P('head'), may hold values from 0.1 to 1.9
- upstream: bfloat16 [8192, 6144], P('seq', 'head'), may hold values from -6 to 6
Outputs:
- attended: bfloat16 [8192, 6144], P('seq', 'head')
- grad_queries: bfloat16 [8192, 6144], P('seq', 'head')
- grad_keys: bfloat16 [8192, 6144], P('seq', 'head')
- grad_values: bfloat16 [8192, 6144], P('seq', 'head')
- grad_gain: float32 [6144], P('head')
The draws below stay inside these ranges and needn't reach their ends.
All inputs are finite; a program needn't handle non-finite values.
Results may differ from the reference program's by a relative error of at most 0.0058.
Values may be sent and summed in bfloat16 or wider, within the bound.
A program may use at most 64 MiB of HBM per device.

```python
import jax
import jax.numpy as jnp
from jax import lax

HEADS = 48
HEAD_DIM = 128
TOK_DEV = 128
TOKENS = 8192


def block_scale(rng, shape, cuts, low, top_value):
    level, own = 1.0, jax.random.fold_in(rng, 6)
    for axis_at, blocks in cuts:
        heights = jnp.exp(jax.random.uniform(jax.random.fold_in(own, axis_at), (blocks,), jnp.float32, low / len(cuts), top_value / len(cuts)))
        level = level * jnp.repeat(heights, shape[axis_at] // blocks).reshape([-1 if axis == axis_at else 1 for axis in range(len(shape))])
    return level


def centred(stream_key, shape, scale, bound, pieces=(), kind=jnp.bfloat16):
    values = scale * jax.random.normal(stream_key, shape, jnp.float32)
    if pieces:
        values = values * block_scale(stream_key, shape, pieces, -0.22, 0.18)
    return jnp.clip(values, -bound, bound).astype(kind)


def setup_inputs(seed: int = 0) -> dict:
    seeds = jax.random.split(jax.random.key(seed), 6)
    return {
        "queries": centred(seeds[0], (TOKENS, HEADS * HEAD_DIM), 1.0, 6.0, ((0, 64), (1, 8))),
        "key_vectors": centred(seeds[1], (TOKENS, HEADS * HEAD_DIM), 1.0, 6.0, ((0, 64), (1, 8))),
        "value_vectors": centred(seeds[2], (TOKENS, HEADS * HEAD_DIM), 1.0, 6.0, ((0, 64), (1, 8))),
        "norm_gain": jnp.clip(1.0 + 0.18 * jax.random.normal(seeds[3], (HEADS * HEAD_DIM,), jnp.float32), 0.1, 1.9),
        "upstream": centred(seeds[4], (TOKENS, HEADS * HEAD_DIM), 1.0, 6.0, ((0, 64), (1, 8))),
    }


def reference(queries, key_vectors, value_vectors, norm_gain, upstream):
    blocks = TOKENS // TOK_DEV
    total_width = HEADS * HEAD_DIM
    shaped = (blocks, TOK_DEV, HEADS, HEAD_DIM)
    query_blocks = queries.reshape(shaped)
    key_blocks = key_vectors.reshape(shaped)
    value_blocks = value_vectors.reshape(shaped)
    upstream_blocks = upstream.reshape(shaped)
    gain_grid = norm_gain.astype(jnp.float32).reshape(HEADS, HEAD_DIM)
    positions = jnp.arange(TOK_DEV, dtype=jnp.int32)
    causal = (positions[None, :] <= positions[:, None])[None]

    def make_state(items):
        return jnp.einsum('thd,the->hde', items[0].astype(jnp.float32), items[1].astype(jnp.float32))
    local_state = lax.map(make_state, (key_blocks, value_blocks))
    running = jnp.cumsum(local_state, axis=0)
    prior = jnp.concatenate([jnp.zeros_like(local_state[:1]), running[:-1]], axis=0).astype(jnp.bfloat16)

    def make_weights(query_b, key_b):
        scores = jnp.einsum('thd,shd->hts', query_b.astype(jnp.float32), key_b.astype(jnp.float32))
        return jnp.where(causal, scores, 0.0).astype(jnp.bfloat16)

    def forward(items):
        query_b, key_b, value_b, prior_b, upstream_b = items
        weights = make_weights(query_b, key_b)
        out = jnp.einsum('hts,she->the', weights.astype(jnp.float32), value_b.astype(jnp.float32))
        out = out + jnp.einsum('thd,hde->the', query_b.astype(jnp.float32), prior_b.astype(jnp.float32))
        inv = lax.rsqrt(lax.optimization_barrier(jnp.sum(out * out, axis=(1, 2))) / total_width + 1e-06)[:, None, None]
        scaled = out * inv
        attended = (scaled * gain_grid).astype(jnp.bfloat16)
        grad_norm = upstream_b.astype(jnp.float32) * gain_grid
        mean_dot = (lax.optimization_barrier(jnp.sum(grad_norm * scaled, axis=(1, 2))) / total_width)[:, None, None]
        d_out = (inv * (grad_norm - scaled * mean_dot)).astype(jnp.bfloat16)
        gain_part = lax.optimization_barrier(jnp.sum(upstream_b.astype(jnp.float32) * scaled, axis=0))
        grad_state = jnp.einsum('thd,the->hde', query_b.astype(jnp.float32), d_out.astype(jnp.float32))
        return (attended, d_out, gain_part, grad_state)
    attended, d_out, gain_parts, grad_state = lax.map(forward, (query_blocks, key_blocks, value_blocks, prior, upstream_blocks))
    backwards = jnp.cumsum(grad_state[::-1], axis=0)[::-1]
    later = jnp.concatenate([backwards[1:], jnp.zeros_like(backwards[:1])], axis=0).astype(jnp.bfloat16)

    def backward(items):
        query_b, key_b, value_b, prior_b, later_b, d_out_b = items
        query_f = query_b.astype(jnp.float32)
        key_f = key_b.astype(jnp.float32)
        value_f = value_b.astype(jnp.float32)
        d_out_f = d_out_b.astype(jnp.float32)
        prior_f = prior_b.astype(jnp.float32)
        later_f = later_b.astype(jnp.float32)
        weights = make_weights(query_b, key_b).astype(jnp.float32)
        d_scores = jnp.where(causal, jnp.einsum('the,she->hts', d_out_f, value_f), 0.0)
        d_scores = d_scores.astype(jnp.bfloat16).astype(jnp.float32)
        grad_q = jnp.einsum('hts,shd->thd', d_scores, key_f) + jnp.einsum('the,hde->thd', d_out_f, prior_f)
        grad_k = jnp.einsum('hts,thd->shd', d_scores, query_f) + jnp.einsum('she,hde->shd', value_f, later_f)
        grad_v = jnp.einsum('hts,the->she', weights, d_out_f) + jnp.einsum('shd,hde->she', key_f, later_f)
        return (grad_q.astype(jnp.bfloat16), grad_k.astype(jnp.bfloat16), grad_v.astype(jnp.bfloat16))
    grad_q, grad_k, grad_v = lax.map(backward, (query_blocks, key_blocks, value_blocks, prior, later, d_out))
    flat = (TOKENS, total_width)
    return (attended.reshape(flat), grad_q.reshape(flat), grad_k.reshape(flat), grad_v.reshape(flat), lax.optimization_barrier(jnp.sum(gain_parts, axis=0)).reshape(total_width))
```

```python
import jax
import jax.numpy as jnp
from jax import lax
from jax.experimental import pallas as pl
from jax.experimental.pallas import tpu as pltpu
from jax.sharding import PartitionSpec as P

HEADS = 48
D = 128
BF = jnp.bfloat16
F32 = jnp.float32
GROUP = 16
GROUP_ORDER = (12, 13, 4, 5, 10, 11, 14, 15, 8, 9, 2, 3, 6, 7, 1)
CROSS = (56, 40, 16)
COLUMN = (32, 40, 24, 56, 16, 48, 8)
ROW = (4, 5, 2, 3, 6, 7, 1)
DEPTH = (4, 3, 5, 2, 6, 1, 7)


def nn(a, b):
    return lax.dot_general(a, b, (((1,), (0,)), ((), ())), preferred_element_type=F32)


def nt(a, b):
    return lax.dot_general(a, b, (((1,), (1,)), ((), ())), preferred_element_type=F32)


def tn(a, b):
    return lax.dot_general(a, b, (((0,), (0,)), ((), ())), preferred_element_type=F32)


def kernel(
    q_hbm, k_hbm, v_hbm, g_hbm, u_hbm,
    at_hbm, gq_hbm, gk_hbm, gv_hbm, gg_hbm,
    q, k, v, g, u, at, gq, gk, gv, gg,
    w, part, out, d_out, keys, vals,
    state, moved, run, total, others, back, whole,
    state2, moved2, run2, total2, others2, back2, whole2,
    norm, norms, gain, gains, gain2, gains2,
    in_sem, out_sem,
    rs_s, rs_r, ex_s, ex_r, ag_s, ag_r,
    rs2_s, rs2_r, ex2_s, ex2_r, ag2_s, ag2_r,
    nm_s, nm_r, c_s, c_r, r_s, r_r,
):
    heads = q_hbm.shape[1] // D
    length = q_hbm.shape[0]
    seq = lax.axis_index("seq")
    head = lax.axis_index("head")
    inner = seq & 15
    outer = seq >> 4
    share = inner ^ ((seq >> 2) & 8)

    loads = [
        pltpu.make_async_copy(a, b, in_sem.at[i])
        for i, (a, b) in enumerate(((k_hbm, k), (v_hbm, v), (q_hbm, q), (u_hbm, u), (g_hbm, g)))
    ]
    for c in loads:
        c.start()

    barrier = pltpu.get_barrier_semaphore()
    peers = sorted(set(GROUP_ORDER) | set(CROSS) | set(COLUMN))
    for m in peers:
        pl.semaphore_signal(barrier, inc=1, device_id={"seq": seq ^ m}, device_id_type=pl.DeviceIdType.MESH)
    for m in DEPTH:
        pl.semaphore_signal(barrier, inc=1, device_id={"head": head ^ m}, device_id_type=pl.DeviceIdType.MESH)

    def send(src, dst, s, r, **where):
        c = pltpu.make_async_remote_copy(
            src_ref=src, dst_ref=dst, send_sem=s, recv_sem=r,
            device_id=where, device_id_type=pl.DeviceIdType.MESH,
        )
        c.start()
        return c

    def cols(h):
        return slice(h * D, (h + 1) * D)

    def scatter(state_ref, moved_ref, s, r):
        copies = []
        for m in GROUP_ORDER:
            copies.append(send(state_ref.at[share ^ m], moved_ref.at[m], s.at[m], r.at[m], seq=seq ^ m))
        moved_ref[0] = state_ref[share]
        return copies

    def cross(copies, moved_ref, total_ref, others_ref, s, r):
        for c in copies:
            c.wait_recv()
        acc = moved_ref[0].astype(F32)
        for m in range(1, GROUP):
            acc = acc + moved_ref[m].astype(F32)
        total_ref[...] = acc.astype(BF)
        return [
            send(total_ref, others_ref.at[i], s.at[i], r.at[i], seq=seq ^ m)
            for i, m in enumerate(CROSS)
        ]

    def running(moved_ref, run_ref, reverse):
        acc = jnp.zeros(run_ref.shape[1:], F32)
        order = range(GROUP - 1, -1, -1) if reverse else range(GROUP)
        for i in order:
            slot = inner ^ i
            run_ref[slot] = acc
            acc = acc + moved_ref[slot].astype(F32)

    def gather(copies, run_ref, others_ref, back_ref, whole_ref, s, r, reverse):
        for c in copies:
            c.wait_recv()
        base = jnp.zeros(run_ref.shape[1:], F32)
        for i, m in enumerate(CROSS):
            peer = outer ^ (m >> 4)
            take = (peer > outer) if reverse else (peer < outer)
            base = base + jnp.where(take, others_ref[i].astype(F32), 0.0)
        sent = []
        for m in GROUP_ORDER:
            back_ref[m] = (run_ref[m] + base).astype(BF)
            sent.append(send(back_ref.at[m], whole_ref.at[share], s.at[m], r.at[m], seq=seq ^ m))
        whole_ref[share] = (run_ref[0] + base).astype(BF)
        return sent

    pend = []
    loads[0].wait()
    loads[1].wait()
    for h in range(heads):
        keys[h * D:(h + 1) * D] = tn(k[:, cols(h)], v[:, cols(h)])
    state[...] = keys[...].astype(BF).reshape(state.shape)
    pl.semaphore_wait(barrier, len(peers) + len(DEPTH))
    first = scatter(state, moved, rs_s, rs_r)
    pend += first

    rows = lax.broadcasted_iota(jnp.int32, (length, length), 0)
    columns = lax.broadcasted_iota(jnp.int32, (length, length), 1)
    causal = columns <= rows
    loads[2].wait()
    for h in range(heads):
        scores = nt(q[:, cols(h)], k[:, cols(h)])
        wh = jnp.where(causal, scores, 0.0).astype(BF)
        w[:, cols(h)] = wh
        part[:, cols(h)] = nn(wh, v[:, cols(h)])
    loads[3].wait()
    loads[4].wait()

    second = cross(first, moved, total, others, ex_s, ex_r)
    pend += second
    running(moved, run, False)
    third = gather(second, run, others, back, whole, ag_s, ag_r, False)
    pend += third
    for c in third:
        c.wait_recv()

    prior = whole[...].reshape(heads * D, D)
    squares = jnp.zeros((length, D), F32)
    crosses = jnp.zeros((length, D), F32)
    for h in range(heads):
        o = part[:, cols(h)] + nn(q[:, cols(h)], prior[h * D:(h + 1) * D])
        out[:, cols(h)] = o
        grad_norm = u[:, cols(h)].astype(F32) * g[pl.ds(h * D, D)][None, :]
        squares = squares + o * o
        crosses = crosses + grad_norm * o
    norm[0:1, :] = jnp.sum(squares.T, axis=0, keepdims=True)
    norm[1:2, :] = jnp.sum(crosses.T, axis=0, keepdims=True)
    fourth = [
        send(norm, norms.at[i], nm_s.at[i], nm_r.at[i], head=head ^ m) for i, m in enumerate(DEPTH)
    ]
    pend += fourth
    for c in fourth:
        c.wait_recv()
    sums = norm[...]
    for i in range(len(DEPTH)):
        sums = sums + norms[i]
    width = HEADS * D
    inv_row = lax.rsqrt(sums[0:1] / width + 1e-06)
    mean_row = sums[1:2] * inv_row / width
    inv = jnp.broadcast_to(inv_row, (D, length)).T
    mean = jnp.broadcast_to(mean_row, (D, length)).T

    for h in range(heads):
        scaled = out[:, cols(h)] * inv
        gh = g[pl.ds(h * D, D)][None, :]
        uf = u[:, cols(h)].astype(F32)
        dh = (inv * (uf * gh - scaled * mean)).astype(BF)
        d_out[:, cols(h)] = dh
        at[:, cols(h)] = (scaled * gh).astype(BF)
        gain[h:h + 1, :] = jnp.sum(uf * scaled, axis=0, keepdims=True)
        keys[h * D:(h + 1) * D] = tn(q[:, cols(h)], dh)
    state2[...] = keys[...].astype(BF).reshape(state2.shape)
    first = scatter(state2, moved2, rs2_s, rs2_r)
    pend += first
    fifth = [
        send(gain, gains.at[i], c_s.at[i], c_r.at[i], seq=seq ^ m) for i, m in enumerate(COLUMN)
    ]
    pend += fifth
    stores = [pltpu.make_async_copy(at, at_hbm, out_sem.at[0])]
    stores[-1].start()

    for h in range(heads):
        dh = d_out[:, cols(h)]
        scores = nt(dh, v[:, cols(h)])
        ds = jnp.where(causal, scores, 0.0).astype(BF)
        part[:, cols(h)] = tn(ds, q[:, cols(h)])
        gq[:, cols(h)] = (nn(ds, k[:, cols(h)]) + nt(dh, prior[h * D:(h + 1) * D])).astype(BF)
    stores.append(pltpu.make_async_copy(gq, gq_hbm, out_sem.at[1]))
    stores[-1].start()

    second = cross(first, moved2, total2, others2, ex2_s, ex2_r)
    pend += second
    running(moved2, run2, True)
    for c in fifth:
        c.wait_recv()
    column = gain[...]
    for i in range(len(COLUMN)):
        column = column + gains[i]
    gain2[...] = column
    sixth = [
        send(gain2, gains2.at[i], r_s.at[i], r_r.at[i], seq=seq ^ m) for i, m in enumerate(ROW)
    ]
    pend += sixth
    third = gather(second, run2, others2, back2, whole2, ag2_s, ag2_r, True)
    pend += third
    for h in range(heads):
        vals[:, cols(h)] = tn(w[:, cols(h)], d_out[:, cols(h)])
    for c in sixth:
        c.wait_recv()
    column = gain2[...]
    for i in range(len(ROW)):
        column = column + gains2[i]
    for h in range(heads):
        gg[pl.ds(h * D, D)] = column[h]
    stores.append(pltpu.make_async_copy(gg, gg_hbm, out_sem.at[2]))
    stores[-1].start()
    for c in third:
        c.wait_recv()
    later = whole2[...].reshape(heads * D, D)
    for h in range(heads):
        lh = later[h * D:(h + 1) * D]
        gk[:, cols(h)] = (part[:, cols(h)] + nt(v[:, cols(h)], lh)).astype(BF)
    stores.append(pltpu.make_async_copy(gk, gk_hbm, out_sem.at[3]))
    stores[-1].start()
    for h in range(heads):
        lh = later[h * D:(h + 1) * D]
        gv[:, cols(h)] = (vals[:, cols(h)] + nn(k[:, cols(h)], lh)).astype(BF)
    stores.append(pltpu.make_async_copy(gv, gv_hbm, out_sem.at[4]))
    stores[-1].start()
    for c in pend:
        c.wait_send()
    for c in stores:
        c.wait()


def body(queries, key_vectors, value_vectors, norm_gain, upstream):
    length, width = queries.shape
    heads = width // D
    rows = heads * D // GROUP
    tall = jax.ShapeDtypeStruct((length, width), BF)
    sem = pltpu.SemaphoreType.DMA

    def scan_buffers():
        return [
            pltpu.VMEM((GROUP, rows, D), BF),
            pltpu.VMEM((GROUP, rows, D), BF),
            pltpu.VMEM((GROUP, rows, D), F32),
            pltpu.VMEM((rows, D), BF),
            pltpu.VMEM((3, rows, D), BF),
            pltpu.VMEM((GROUP, rows, D), BF),
            pltpu.VMEM((GROUP, rows, D), BF),
        ]

    def scan_sems():
        return [sem((GROUP,)), sem((GROUP,)), sem((3,)), sem((3,)), sem((GROUP,)), sem((GROUP,))]

    return pl.pallas_call(
        kernel,
        out_shape=(tall, tall, tall, tall, jax.ShapeDtypeStruct((width,), F32)),
        in_specs=[pl.BlockSpec(memory_space=pl.ANY)] * 5,
        out_specs=[pl.BlockSpec(memory_space=pl.ANY)] * 5,
        scratch_shapes=[
            pltpu.VMEM((length, width), BF),
            pltpu.VMEM((length, width), BF),
            pltpu.VMEM((length, width), BF),
            pltpu.VMEM((width,), F32),
            pltpu.VMEM((length, width), BF),
            pltpu.VMEM((length, width), BF),
            pltpu.VMEM((length, width), BF),
            pltpu.VMEM((length, width), BF),
            pltpu.VMEM((length, width), BF),
            pltpu.VMEM((width,), F32),
            pltpu.VMEM((length, width), BF),
            pltpu.VMEM((length, width), F32),
            pltpu.VMEM((length, width), F32),
            pltpu.VMEM((length, width), BF),
            pltpu.VMEM((width, D), F32),
            pltpu.VMEM((length, width), F32),
            *scan_buffers(),
            *scan_buffers(),
            pltpu.VMEM((2, D), F32),
            pltpu.VMEM((7, 2, D), F32),
            pltpu.VMEM((heads, D), F32),
            pltpu.VMEM((7, heads, D), F32),
            pltpu.VMEM((heads, D), F32),
            pltpu.VMEM((7, heads, D), F32),
            sem((5,)),
            sem((5,)),
            *scan_sems(),
            *scan_sems(),
            sem((7,)), sem((7,)), sem((7,)), sem((7,)), sem((7,)), sem((7,)),
        ],
        compiler_params=pltpu.CompilerParams(collective_id=0, has_side_effects=True),
    )(queries, key_vectors, value_vectors, norm_gain, upstream)


def solution(mesh):
    tall = P("seq", "head")
    return jax.shard_map(
        body,
        mesh=mesh,
        in_specs=(tall, tall, tall, P("head"), tall),
        out_specs=(tall, tall, tall, tall, P("head")),
        check_vma=False,
    )
```
